32 devices in a mesh: gz: 4 (over z), lat: 8 (over y, x, core).
Axes of the slice: x: 2, y: 2, z: 4, core: 2. Of those that a mesh axis runs over, the one named last changes fastest.
Arguments:
- features: bfloat16 [8, 512, 1536], P('lat', 'gz'), may hold values from -6 to 6
- input_map: bfloat16 [8, 512, 128], P('lat', 'gz'), may hold values from -0.5 to 0.5
- output_map: bfloat16 [8, 512, 128], P('lat', 'gz'), may hold values from -0.5 to 0.5
- step_size: float32 [8, 512, 24], P('lat', 'gz'), may hold values from 0.008 to 0.11, as said below
- decay_rate: float32 [24], replicated, may hold values from 0.005859375 to 1, as said below
- skip_gain: float32 [24], replicated, may hold values from 0.5 to 1.5
- kernel: float32 [3, 1536], replicated, may hold values from -2.5 to 2.5
- cotangent: bfloat16 [8, 512, 1536], P(None, ('gz', 'lat')), may hold values from -23 to 23
Outputs:
- lateral_out: bfloat16 [8, 512, 1536], P(None, ('gz', 'lat'))
- grad_features: bfloat16 [8, 512, 1536], P('lat', 'gz')
- grad_input_map: bfloat16 [8, 512, 128], P('lat', 'gz')
- grad_output_map: bfloat16 [8, 512, 128], P('lat', 'gz')
- grad_kernel: float32 [3, 1536], replicated
The draws below stay inside these ranges and needn't reach their ends.
Inputs may be any that keep to these rules, and one draw needn't show every extreme that they name: `step_size`: positive step sizes. `decay_rate`: positive rates.
All inputs are finite; a program needn't handle non-finite values.
Results may differ from the reference program's by a relative error of at most 0.0069.
Values may be sent and summed in bfloat16 or wider, within the bound.
A program may use at most 128 MiB of HBM per device.

```python
import math
from functools import partial
import jax
import jax.numpy as jnp
from jax import lax

H = 24
P_SIZE = 64
NS = 128
KW = 3
SEC_DEV = 128
HP = 1536
Z = 512
LX = 8


def draw_decay_rate(key, part):
    pick_key, level_key = jax.random.split(key)
    fraction = 0.5
    is_fast = jax.random.bernoulli(pick_key, fraction, (H,))
    levels = jax.random.uniform(level_key, (H,), jnp.float32)
    fast_rate = 0.5 * 2.0 ** levels
    slow_rate = 0.1 * 6.0 ** levels / (0.03 * Z)
    return jnp.where(is_fast, fast_rate, slow_rate).astype(jnp.float32)


def draw_step_size(key, part):
    jitter_key, block_key = jax.random.split(key)
    levels = jax.random.uniform(jitter_key, (LX, Z, H), jnp.float32)
    jitter = 0.5 * 4.0 ** levels
    blocks = jax.random.uniform(block_key, (LX, Z // SEC_DEV, 1, H), jnp.float32)
    factor = 0.6 * (1.7 / 0.6) ** blocks
    factor = jnp.broadcast_to(factor, (LX, Z // SEC_DEV, SEC_DEV, H)).reshape(LX, Z, H)
    return (0.03 * jitter * factor).astype(jnp.float32)


def draw_cotangent(key, part):
    noise_key, row_key = jax.random.split(key)
    noise = jnp.clip(jax.random.normal(noise_key, (LX, Z, HP), jnp.float32), -4.0, 4.0)
    row_scale = 0.4 * 6.25 ** jax.random.uniform(row_key, (LX, Z, 1), jnp.float32)
    across = 0.5 + jnp.arange(LX, dtype=jnp.float32) / LX
    along_sections = 0.5 + jnp.arange(Z, dtype=jnp.float32) / Z
    return (noise * row_scale * across[:, None, None] * along_sections[None, :, None]).astype(jnp.bfloat16)


def block_levels(stream_key, dims, cuts, low, high):
    factor_of, own = 1.0, jax.random.fold_in(stream_key, 6)
    for position, blocks in cuts:
        heights = jnp.exp(jax.random.uniform(jax.random.fold_in(own, position), (blocks,), jnp.float32, low / len(cuts), high / len(cuts)))
        factor_of = factor_of * jnp.repeat(heights, dims[position] // blocks).reshape([-1 if axis == position else 1 for axis in range(len(dims))])
    return factor_of


def centred(rng, shape, width, bound, cuts=(), held_as=jnp.bfloat16):
    array = jax.random.normal(rng, shape, jnp.float32) * width
    if len(cuts) > 0:
        array = block_levels(rng, shape, cuts, -0.22, 0.18) * array
    return jnp.clip(array, min=-bound, max=bound).astype(held_as)


def setup_inputs(seed: int = 0) -> dict:
    keys = jax.random.split(jax.random.key(seed), 9)
    return {
        "features": centred(keys[0], (LX, Z, HP), 1.0, 6.0, ((0, 8), (1, 4))),
        "input_map": centred(keys[1], (LX, Z, NS), NS ** -0.5, 0.5, ((0, 8), (1, 4))),
        "output_map": centred(keys[2], (LX, Z, NS), NS ** -0.5, 0.5, ((0, 8), (1, 4))),
        "step_size": draw_step_size(jax.random.fold_in(keys[8], 71), 0),
        "decay_rate": draw_decay_rate(jax.random.fold_in(keys[8], 71), 0),
        "skip_gain": jnp.clip(jax.random.uniform(keys[5], (H,), jnp.float32, 0.5, 1.5), 0.5, 1.5),
        "kernel": centred(keys[6], (KW, HP), 0.5, 2.5, (), jnp.float32),
        "cotangent": draw_cotangent(jax.random.fold_in(keys[8], 71), 0),
    }


def decay_head(log_decay, step_head):
    length = log_decay.shape[0]
    row_index = lax.broadcasted_iota(jnp.int32, (length, length), 0)
    col_index = lax.broadcasted_iota(jnp.int32, (length, length), 1)
    spread = log_decay[:, None] - log_decay[None, :]
    return jnp.exp(jnp.where(row_index >= col_index, spread, -jnp.inf)) * step_head[None, :]

def local_terms(input_block, output_block, step_block, decay_rate):
    log_decay = jnp.cumsum(-step_block * decay_rate[None, :], axis=0)
    block_total = log_decay[-1]
    out_weight = step_block * jnp.exp(block_total[None, :] - log_decay)
    map_product = jnp.dot(output_block, input_block.T, preferred_element_type=jnp.float32)
    decay_mask = jax.vmap(decay_head, in_axes=(1, 1))(log_decay, step_block)
    mix_weights = (map_product[None] * decay_mask).astype(jnp.bfloat16)
    in_weights = (input_block.astype(jnp.float32)[:, None, :] * out_weight[:, :, None]).astype(jnp.bfloat16)
    out_read = (output_block.astype(jnp.float32)[:, None, :] * jnp.exp(log_decay)[:, :, None]).astype(jnp.bfloat16)
    return (log_decay, block_total, out_weight, decay_mask, mix_weights, in_weights, out_read)

def forward_block(running, pieces, decay_rate, skip_gain):
    features, input_block, output_block, step_block = pieces
    length, channels = features.shape
    head_count = step_block.shape[1]
    head_size = channels // head_count
    log_decay, block_total, out_weight, decay_mask, mix_weights, in_weights, out_read = local_terms(input_block, output_block, step_block, decay_rate)
    heads_in = features.reshape(length, head_count, head_size).astype(jnp.float32)
    state_low = running.astype(jnp.bfloat16)
    within = jnp.einsum('hji,ihp->jhp', mix_weights.astype(jnp.float32), heads_in)
    carried = jnp.einsum('jhn,hpn->jhp', out_read.astype(jnp.float32), state_low.astype(jnp.float32))
    ssd_out = (within + carried + skip_gain[None, :, None] * heads_in).reshape(length, channels).astype(jnp.bfloat16)
    block_state = jnp.einsum('ihp,ihn->hpn', heads_in, in_weights.astype(jnp.float32))
    updated = jnp.exp(block_total)[:, None, None] * running + block_state
    return (updated, (ssd_out, state_low))

def backward_block(running, pieces, decay_rate, skip_gain):
    features, input_block, output_block, step_block, grad_block, state_low = pieces
    length, channels = features.shape
    head_count = step_block.shape[1]
    head_size = channels // head_count
    log_decay, block_total, out_weight, decay_mask, mix_weights, in_weights, out_read = local_terms(input_block, output_block, step_block, decay_rate)
    heads_in = features.reshape(length, head_count, head_size).astype(jnp.float32)
    heads_grad = grad_block.reshape(length, head_count, head_size).astype(jnp.float32)
    adjoint_low = running.astype(jnp.bfloat16)
    grad_feat = jnp.einsum('hji,jhp->ihp', mix_weights.astype(jnp.float32), heads_grad)
    grad_feat = grad_feat + jnp.einsum('ihn,hpn->ihp', in_weights.astype(jnp.float32), adjoint_low.astype(jnp.float32))
    grad_feat = (grad_feat + skip_gain[None, :, None] * heads_grad).reshape(length, channels).astype(jnp.bfloat16)
    block_adjoint = jnp.einsum('jhn,jhp->hpn', out_read.astype(jnp.float32), heads_grad)
    pair_inner = jnp.einsum('jhp,ihp->hji', heads_grad, heads_in)
    pair_weights = lax.optimization_barrier(jnp.sum(pair_inner * decay_mask, axis=0)).astype(jnp.bfloat16)
    grad_read = (heads_grad * jnp.exp(log_decay)[:, :, None]).astype(jnp.bfloat16).reshape(length, channels)
    feat_weights = (heads_in * out_weight[:, :, None]).astype(jnp.bfloat16).reshape(length, channels)
    state_rows = state_low.reshape(channels, -1)
    adjoint_rows = adjoint_low.reshape(channels, -1)
    grad_out_map = jnp.dot(pair_weights, input_block, preferred_element_type=jnp.float32)
    grad_out_map = (grad_out_map + jnp.dot(grad_read, state_rows, preferred_element_type=jnp.float32)).astype(jnp.bfloat16)
    grad_in_map = jnp.dot(pair_weights.T, output_block, preferred_element_type=jnp.float32)
    grad_in_map = (grad_in_map + jnp.dot(feat_weights, adjoint_rows, preferred_element_type=jnp.float32)).astype(jnp.bfloat16)
    updated = jnp.exp(block_total)[:, None, None] * running + block_adjoint
    return (updated, (grad_feat, grad_in_map, grad_out_map))

def lateral_sum(padded, kernel, extent, flip):
    tap_count = kernel.shape[0]
    summed = 0.0
    for tap_index in range(tap_count):
        anchor = tap_count - 1 - tap_index if flip else tap_index
        summed = summed + kernel[tap_index][None, None, :] * padded[anchor:anchor + extent]
    return summed

def kernel_terms(cotangent, padded, extent, tap_count):
    cot_wide = cotangent.astype(jnp.float32)
    return jnp.stack([jnp.einsum('xzc,xzc->c', cot_wide, padded[tap_index:tap_index + extent].astype(jnp.float32)) for tap_index in range(tap_count)])

def reference(features, input_map, output_map, step_size, decay_rate, skip_gain, kernel, cotangent):
    blocks = Z // SEC_DEV
    margin = KW // 2
    forward_step = partial(forward_block, decay_rate=decay_rate, skip_gain=skip_gain)
    backward_step = partial(backward_block, decay_rate=decay_rate, skip_gain=skip_gain)

    def column_forward(column):
        feat_col, in_col, out_col, step_col = column
        pieces = (feat_col.reshape(blocks, SEC_DEV, HP), in_col.reshape(blocks, SEC_DEV, NS), out_col.reshape(blocks, SEC_DEV, NS), step_col.reshape(blocks, SEC_DEV, H))
        unused, (ssd_col, state_col) = lax.scan(forward_step, jnp.zeros((H, P_SIZE, NS), jnp.float32), pieces)
        return (ssd_col.reshape(Z, HP), state_col)
    ssd_out, state_low = lax.map(column_forward, (features, input_map, output_map, step_size))
    widths = ((margin, margin), (0, 0), (0, 0))
    padded_out = jnp.pad(ssd_out, widths)
    lateral_out = lateral_sum(padded_out, kernel, LX, False).astype(jnp.bfloat16)
    grad_ssd = lateral_sum(jnp.pad(cotangent, widths), kernel, LX, True).astype(jnp.bfloat16)
    grad_kernel = kernel_terms(cotangent, padded_out, LX, KW) / math.sqrt(LX * Z)

    def column_backward(column):
        feat_col, in_col, out_col, step_col, grad_col, state_col = column
        pieces = (feat_col.reshape(blocks, SEC_DEV, HP), in_col.reshape(blocks, SEC_DEV, NS), out_col.reshape(blocks, SEC_DEV, NS), step_col.reshape(blocks, SEC_DEV, H), grad_col.reshape(blocks, SEC_DEV, HP), state_col)
        unused, (grad_feat, grad_in, grad_out) = lax.scan(backward_step, jnp.zeros((H, P_SIZE, NS), jnp.float32), pieces, reverse=True)
        return (grad_feat.reshape(Z, HP), grad_in.reshape(Z, NS), grad_out.reshape(Z, NS))
    grad_features, grad_input_map, grad_output_map = lax.map(column_backward, (features, input_map, output_map, step_size, grad_ssd, state_low))
    return (lateral_out, grad_features, grad_input_map, grad_output_map, grad_kernel)
```

```python
import functools
import math

import jax
import jax.numpy as jnp
from jax import lax
from jax.experimental import pallas as pl
from jax.experimental.pallas import tpu as pltpu
from jax.sharding import PartitionSpec as P

F32 = jnp.float32
BF16 = jnp.bfloat16
MESH = pl.DeviceIdType.MESH
HOP_STEPS = 2
LATE_STEPS = 3


def dot(a, b, da, db):
    return lax.dot_general(a, b, (((da,), (db,)), ((), ())), preferred_element_type=F32)


def expand(values, onehot):
    high = values.astype(BF16)
    low = (values - high.astype(F32)).astype(BF16)
    return dot(high, onehot, 1, 0) + dot(low, onehot, 1, 0)


def kernel_body(
    gz_count, lat_count, width, row_total,
    feat_hbm, in_ref, out_ref, step_ref, rate_ref, skip_ref, ker_ref, cot_hbm,
    lat_ref, gf_ref, gim_ref, gom_ref, gk_ref,
    feat, cotp, gsend, grecv, osend, orecv, wide,
    fw, gr, grad, ec, wc, within, bs, ad, sin, sout, ain, aout, sp, ap, vecs, gk1, gk2,
    load_sem, gs_sem, gr_sem, os_sem, or_sem, fs_sem, fr_sem, bs_sem, br_sem, k_sem,
):
    gz = lax.axis_index("gz")
    me = lax.axis_index("lat")
    sections, channels = feat.shape
    heads = step_ref.shape[1]
    head_size = channels // heads
    rows = gsend.shape[1]
    taps = ker_ref.shape[0]
    chunks = channels // width
    aligned = rows % 16 == 0

    load_cot = pltpu.make_async_copy(cot_hbm, cotp.at[pl.ds(1, lat_count)], load_sem.at[0])
    load_feat = pltpu.make_async_copy(feat_hbm.at[0], feat, load_sem.at[1])
    load_cot.start()
    load_feat.start()

    barrier = pltpu.get_barrier_semaphore()

    def greet_lat(step, carry):
        pl.semaphore_signal(
            barrier, inc=1, device_id=(gz, lax.rem(me + step, lat_count)), device_id_type=MESH
        )
        return carry

    def greet_gz(step, carry):
        pl.semaphore_signal(
            barrier, inc=1, device_id=(lax.rem(gz + step, gz_count), me), device_id_type=MESH
        )
        return carry

    lax.fori_loop(1, lat_count, greet_lat, 0)
    lax.fori_loop(1, gz_count, greet_gz, 0)

    zero_plane = jnp.zeros((rows, channels), BF16)
    cotp[0] = zero_plane
    cotp[lat_count + 1] = zero_plane
    orecv[0] = zero_plane
    orecv[lat_count + 1] = zero_plane

    load_cot.wait()

    def grad_plane(x, carry):
        total = ker_ref[0:1, :] * cotp[x + 2].astype(F32)
        for tap in range(1, taps):
            total = total + ker_ref[tap : tap + 1, :] * cotp[x + 2 - tap].astype(F32)
        gsend[x] = total.astype(BF16)
        return carry

    lax.fori_loop(0, lat_count, grad_plane, 0, unroll=lat_count <= 8)
    pl.semaphore_wait(barrier, lat_count + gz_count - 2)

    def grad_copy(dest):
        return pltpu.make_async_remote_copy(
            src_ref=gsend.at[dest], dst_ref=grecv.at[me], send_sem=gs_sem, recv_sem=gr_sem,
            device_id=(gz, dest), device_id_type=MESH,
        )

    def grad_start(step, carry):
        grad_copy(lax.rem(me + step, lat_count)).start()
        return carry

    lax.fori_loop(1, lat_count, grad_start, 0)
    grecv[me] = gsend[me]

    row_index = lax.broadcasted_iota(jnp.int32, (sections, sections), 0)
    col_index = lax.broadcasted_iota(jnp.int32, (sections, sections), 1)
    lower = row_index >= col_index
    step_size = step_ref[...]
    log_decay = lax.dot_general(
        jnp.where(lower, 1.0, 0.0), -step_size * rate_ref[...], (((1,), (0,)), ((), ())),
        preferred_element_type=F32, precision=lax.Precision.HIGHEST,
    )
    middle = log_decay[sections // 2 - 1 : sections // 2]
    last = log_decay[sections - 1 : sections]
    head_index = lax.broadcasted_iota(jnp.int32, (heads, channels), 0)
    lane_index = lax.broadcasted_iota(jnp.int32, (heads, channels), 1)
    low_lane = head_index * head_size
    onehot = jnp.where(
        (lane_index >= low_lane) & (lane_index < low_lane + head_size), 1.0, 0.0
    ).astype(BF16)
    wc[...] = expand(step_size * jnp.exp(middle - log_decay), onehot)
    which = lax.broadcasted_iota(jnp.int32, (8, heads), 0)
    vectors = jnp.where(
        which == 0,
        jnp.exp(middle),
        jnp.where(which == 1, jnp.exp(last), jnp.where(which == 2, jnp.exp(last - middle), skip_ref[...])),
    )
    vecs[...] = expand(vectors, onehot)
    load_feat.wait()
    fw[...] = (wc[...] * feat[...].astype(F32)).astype(BF16)
    in_map = in_ref[...]
    out_map = out_ref[...]
    in_turned = in_map.astype(F32).T.astype(BF16)
    out_turned = out_map.astype(F32).T.astype(BF16)
    bs[...] = dot(in_turned, fw[...], 1, 0) * vecs[2:3, :]
    product = jnp.where(lower, dot(out_map, in_map, 1, 1), 0.0)
    mix = product.astype(BF16)
    mix_turned = product.T.astype(BF16)

    def forward_copy(c):
        return pltpu.make_async_remote_copy(
            src_ref=sout.at[c], dst_ref=sin.at[c], send_sem=fs_sem.at[c], recv_sem=fr_sem.at[c],
            device_id=(lax.rem(gz + 1, gz_count), me), device_id_type=MESH,
        )

    def backward_copy(c):
        return pltpu.make_async_remote_copy(
            src_ref=aout.at[c], dst_ref=ain.at[c], send_sem=bs_sem.at[c], recv_sem=br_sem.at[c],
            device_id=(lax.rem(gz + gz_count - 1, gz_count), me), device_id_type=MESH,
        )

    def out_copy(c, lanes, dest):
        return pltpu.make_async_remote_copy(
            src_ref=osend.at[dest, :, lanes], dst_ref=orecv.at[me + 1, :, lanes],
            send_sem=os_sem.at[c], recv_sem=or_sem.at[c],
            device_id=(gz, dest), device_id_type=MESH,
        )

    def span(c):
        return pl.ds(pl.multiple_of(c * width, width), width)

    def first_use():
        ec[...] = expand(jnp.exp(log_decay - middle), onehot)
        within[...] = dot(mix, fw[...], 1, 0)

    def gradients():
        pltpu.make_async_remote_copy(
            src_ref=gsend.at[pl.ds(0, lat_count - 1)], dst_ref=grecv.at[pl.ds(0, lat_count - 1)],
            send_sem=gs_sem, recv_sem=gr_sem, device_id=(gz, me), device_id_type=MESH,
        ).wait_recv()
        if aligned:
            grad[...] = grecv[...].reshape(sections, channels).astype(F32)
        else:
            for source in range(lat_count):
                grad[source * rows : (source + 1) * rows, :] = grecv[source].astype(F32)
        gr[...] = (ec[...] * grad[...]).astype(BF16)
        ad[...] = dot(out_turned, gr[...], 1, 0) * vecs[0:1, :]

    def forward_chunk(c):
        lanes = span(c)

        @pl.when(gz > 0)
        def _():
            forward_copy(c).wait_recv()

        @pl.when(gz == 0)
        def _():
            sin[c] = jnp.zeros((sin.shape[1], width), BF16)

        state = sin[c].astype(F32)

        @pl.when(gz < gz_count - 1)
        def _():
            sout[c] = (state * vecs[1:2, lanes] + bs[:, lanes]).astype(BF16)
            forward_copy(c).start()

        low = (state * vecs[0:1, lanes]).astype(BF16)
        sp[:, lanes] = low
        total = ec[:, lanes] * (within[:, lanes] + dot(out_map, low, 1, 0))
        total = total + vecs[3:4, lanes] * feat[:, lanes].astype(F32)
        if aligned:
            osend[:, :, lanes] = total.astype(BF16).reshape(lat_count, rows, width)
        else:
            wide[...] = total
            for dest in range(lat_count):
                osend[dest, :, lanes] = wide[dest * rows : (dest + 1) * rows, :].astype(BF16)

        def start(step, carry):
            out_copy(c, lanes, lax.rem(me + step, lat_count)).start()
            return carry

        lax.fori_loop(1, lat_count, start, 0)
        orecv[me + 1, :, lanes] = osend[me, :, lanes]

    def backward_chunk(c):
        lanes = span(c)

        @pl.when(gz < gz_count - 1)
        def _():
            backward_copy(c).wait_recv()

        @pl.when(gz == gz_count - 1)
        def _():
            ain[c] = jnp.zeros((ain.shape[1], width), BF16)

        state = ain[c].astype(F32)

        @pl.when(gz > 0)
        def _():
            aout[c] = (state * vecs[1:2, lanes] + ad[:, lanes]).astype(BF16)
            backward_copy(c).start()

        ap[:, lanes] = (state * vecs[2:3, lanes]).astype(BF16)

    first_use()

    def tick(step, carry):
        c = step - gz * HOP_STEPS

        @pl.when((c >= 0) & (c < chunks))
        def _():
            forward_chunk(c)

        @pl.when(step == LATE_STEPS)
        def _():
            gradients()

        e = step - LATE_STEPS - (gz_count - 1 - gz) * HOP_STEPS

        @pl.when((e >= 0) & (e < chunks))
        def _():
            backward_chunk(e)

        return carry

    lax.fori_loop(0, chunks + LATE_STEPS + (gz_count - 1) * HOP_STEPS, tick, 0)

    def plane_chunk(c, carry):
        lanes = span(c)
        pltpu.make_async_remote_copy(
            src_ref=osend.at[pl.ds(0, lat_count - 1), :, lanes],
            dst_ref=orecv.at[pl.ds(1, lat_count - 1), :, lanes],
            send_sem=os_sem.at[c], recv_sem=or_sem.at[c], device_id=(gz, me), device_id_type=MESH,
        ).wait_recv()

        def plane(x, sums):
            cot = cotp[x + 1, :, lanes].astype(F32)
            total = 0.0
            new = []
            for tap in range(taps):
                piece = orecv[x + tap, :, lanes].astype(F32)
                total = total + ker_ref[tap : tap + 1, lanes] * piece
                new.append(sums[tap] + cot * piece)
            lat_ref[x, :, lanes] = total.astype(BF16)
            return tuple(new)

        sums = lax.fori_loop(
            0, lat_count, plane, tuple(jnp.zeros((rows, width), F32) for _ in range(taps)),
            unroll=lat_count <= 8,
        )
        for tap in range(taps):
            gk1[me, tap : tap + 1, lanes] = jnp.sum(sums[tap], axis=0, keepdims=True)
        return carry

    lax.fori_loop(0, chunks, plane_chunk, 0)

    def lat_start(step, carry):
        pltpu.make_async_remote_copy(
            src_ref=gk1.at[me], dst_ref=gk1.at[me], send_sem=k_sem.at[0], recv_sem=k_sem.at[1],
            device_id=(gz, lax.rem(me + step, lat_count)), device_id_type=MESH,
        ).start()
        return carry

    lax.fori_loop(1, lat_count, lat_start, 0)

    pair = jnp.where(lower, dot(gr[...], fw[...], 1, 1), 0.0)
    gom = dot(pair.astype(BF16), in_map, 1, 0) + dot(gr[...], sp[...], 1, 1)
    gom_ref[...] = gom.astype(BF16)

    lat_all = pltpu.make_async_remote_copy(
        src_ref=gk1.at[pl.ds(0, lat_count - 1)], dst_ref=gk1.at[pl.ds(0, lat_count - 1)],
        send_sem=k_sem.at[0], recv_sem=k_sem.at[1], device_id=(gz, me), device_id_type=MESH,
    )
    lat_all.wait_recv()
    gk2[gz] = jnp.sum(gk1[...], axis=0)

    def gz_start(step, carry):
        pltpu.make_async_remote_copy(
            src_ref=gk2.at[gz], dst_ref=gk2.at[gz], send_sem=k_sem.at[2], recv_sem=k_sem.at[3],
            device_id=(lax.rem(gz + step, gz_count), me), device_id_type=MESH,
        ).start()
        return carry

    lax.fori_loop(1, gz_count, gz_start, 0)

    gim = dot(pair.T.astype(BF16), out_map, 1, 0) + dot(fw[...], ap[...], 1, 1)
    gim_ref[...] = gim.astype(BF16)
    gf = dot(mix_turned, gr[...], 1, 0) + dot(in_map, ap[...], 1, 0)
    gf_ref[...] = (wc[...] * gf + vecs[3:4, :] * grad[...]).astype(BF16)

    gz_all = pltpu.make_async_remote_copy(
        src_ref=gk2.at[pl.ds(0, gz_count - 1)], dst_ref=gk2.at[pl.ds(0, gz_count - 1)],
        send_sem=k_sem.at[2], recv_sem=k_sem.at[3], device_id=(gz, me), device_id_type=MESH,
    )
    gz_all.wait_recv()
    gk_ref[...] = jnp.sum(gk2[...], axis=0) * (1.0 / math.sqrt(row_total))

    lat_all.wait_send()
    gz_all.wait_send()
    pltpu.make_async_remote_copy(
        src_ref=gsend.at[pl.ds(0, lat_count - 1)], dst_ref=grecv.at[pl.ds(0, lat_count - 1)],
        send_sem=gs_sem, recv_sem=gr_sem, device_id=(gz, me), device_id_type=MESH,
    ).wait_send()

    def drain(c, carry):
        lanes = span(c)
        pltpu.make_async_remote_copy(
            src_ref=osend.at[pl.ds(0, lat_count - 1), :, lanes],
            dst_ref=orecv.at[pl.ds(1, lat_count - 1), :, lanes],
            send_sem=os_sem.at[c], recv_sem=or_sem.at[c], device_id=(gz, me), device_id_type=MESH,
        ).wait_send()

        @pl.when(gz < gz_count - 1)
        def _():
            forward_copy(c).wait_send()

        @pl.when(gz > 0)
        def _():
            backward_copy(c).wait_send()

        return carry

    lax.fori_loop(0, chunks, drain, 0)


def per_device(
    features, input_map, output_map, step_size, decay_rate, skip_gain, kernel, cotangent
):
    columns, sections, channels = features.shape
    assert columns == 1
    heads = step_size.shape[2]
    states = input_map.shape[2]
    taps = kernel.shape[0]
    assert taps == 3
    gz_count = lax.axis_size("gz")
    lat_count = lax.axis_size("lat")
    extent, rows, _ = cotangent.shape
    assert extent == lat_count
    width = 256
    chunks = channels // width
    row_total = columns * sections * gz_count * lat_count
    vmem = pl.BlockSpec(memory_space=pltpu.VMEM)
    hbm = pl.BlockSpec(memory_space=pl.ANY)
    full = (sections, channels)
    turned = (states, channels)
    lateral_out, grad_features, grad_in, grad_out, grad_kernel = pl.pallas_call(
        functools.partial(kernel_body, gz_count, lat_count, width, row_total),
        out_shape=(
            jax.ShapeDtypeStruct(cotangent.shape, BF16),
            jax.ShapeDtypeStruct(full, BF16),
            jax.ShapeDtypeStruct((sections, states), BF16),
            jax.ShapeDtypeStruct((sections, states), BF16),
            jax.ShapeDtypeStruct((taps, channels), F32),
        ),
        in_specs=[hbm, vmem, vmem, vmem, vmem, vmem, vmem, hbm],
        out_specs=(vmem,) * 5,
        scratch_shapes=[
            pltpu.VMEM(full, BF16),
            pltpu.VMEM((extent + 2, rows, channels), BF16),
            pltpu.VMEM((lat_count, rows, channels), BF16),
            pltpu.VMEM((lat_count, rows, channels), BF16),
            pltpu.VMEM((lat_count, rows, channels), BF16),
            pltpu.VMEM((extent + 2, rows, channels), BF16),
            pltpu.VMEM((sections, width), F32),
            pltpu.VMEM(full, BF16),
            pltpu.VMEM(full, BF16),
            pltpu.VMEM(full, F32),
            pltpu.VMEM(full, F32),
            pltpu.VMEM(full, F32),
            pltpu.VMEM(full, F32),
            pltpu.VMEM(turned, F32),
            pltpu.VMEM(turned, F32),
            pltpu.VMEM((chunks, states, width), BF16),
            pltpu.VMEM((chunks, states, width), BF16),
            pltpu.VMEM((chunks, states, width), BF16),
            pltpu.VMEM((chunks, states, width), BF16),
            pltpu.VMEM(turned, BF16),
            pltpu.VMEM(turned, BF16),
            pltpu.VMEM((8, channels), F32),
            pltpu.VMEM((lat_count, taps, channels), F32),
            pltpu.VMEM((gz_count, taps, channels), F32),
            pltpu.SemaphoreType.DMA((2,)),
            pltpu.SemaphoreType.DMA,
            pltpu.SemaphoreType.DMA,
            pltpu.SemaphoreType.DMA((chunks,)),
            pltpu.SemaphoreType.DMA((chunks,)),
            pltpu.SemaphoreType.DMA((chunks,)),
            pltpu.SemaphoreType.DMA((chunks,)),
            pltpu.SemaphoreType.DMA((chunks,)),
            pltpu.SemaphoreType.DMA((chunks,)),
            pltpu.SemaphoreType.DMA((4,)),
        ],
        compiler_params=pltpu.CompilerParams(collective_id=0, has_side_effects=True),
    )(
        features,
        input_map.reshape(sections, states),
        output_map.reshape(sections, states),
        step_size.reshape(sections, heads),
        decay_rate.reshape(1, heads),
        skip_gain.reshape(1, heads),
        kernel,
        cotangent,
    )
    return (
        lateral_out,
        grad_features.reshape(features.shape),
        grad_in.reshape(input_map.shape),
        grad_out.reshape(output_map.shape),
        grad_kernel,
    )


def solution(mesh):
    in_specs = (
        P("lat", "gz", None),
        P("lat", "gz", None),
        P("lat", "gz", None),
        P("lat", "gz", None),
        P(),
        P(),
        P(),
        P(None, ("gz", "lat"), None),
    )
    out_specs = (
        P(None, ("gz", "lat"), None),
        P("lat", "gz", None),
        P("lat", "gz", None),
        P("lat", "gz", None),
        P(),
    )
    return jax.shard_map(
        per_device, mesh=mesh, in_specs=in_specs, out_specs=out_specs, check_vma=False
    )
```

```python
import functools
import math

import jax
import jax.numpy as jnp
from jax import lax
from jax.experimental import pallas as pl
from jax.experimental.pallas import tpu as pltpu
from jax.sharding import PartitionSpec as P

F32 = jnp.float32
BF16 = jnp.bfloat16
MESH = pl.DeviceIdType.MESH
HOP_STEPS = 2
LATE_STEPS = 3


def dot(a, b, da, db):
    return lax.dot_general(a, b, (((da,), (db,)), ((), ())), preferred_element_type=F32)


def expand(values, onehot):
    high = values.astype(BF16)
    low = (values - high.astype(F32)).astype(BF16)
    return dot(high, onehot, 1, 0) + dot(low, onehot, 1, 0)


def kernel_body(
    gz_count, lat_count, width, row_total,
    feat_hbm, in_ref, out_ref, step_ref, rate_ref, skip_ref, ker_ref, cot_hbm,
    lat_ref, gf_ref, gim_ref, gom_ref, gk_ref,
    feat, cotp, gsend, grecv, osend, orecv, wide,
    fw, gr, grad, ec, wc, within, bs, ad, sin, sout, ain, aout, sp, ap, vecs, gk1, gk2,
    load_sem, gs_sem, gr_sem, os_sem, or_sem, fs_sem, fr_sem, bs_sem, br_sem, k_sem,
):
    gz = lax.axis_index("gz")
    me = lax.axis_index("lat")
    sections, channels = feat.shape
    heads = step_ref.shape[0]
    head_size = channels // heads
    rows = gsend.shape[1]
    taps = ker_ref.shape[0]
    chunks = channels // width
    aligned = rows % 16 == 0

    load_cot = pltpu.make_async_copy(cot_hbm, cotp.at[pl.ds(1, lat_count)], load_sem.at[0])
    load_feat = pltpu.make_async_copy(feat_hbm.at[0], feat, load_sem.at[1])
    load_cot.start()
    load_feat.start()

    barrier = pltpu.get_barrier_semaphore()

    def greet_lat(step, carry):
        pl.semaphore_signal(
            barrier, inc=1, device_id=(gz, lax.rem(me + step, lat_count)), device_id_type=MESH
        )
        return carry

    def greet_gz(step, carry):
        pl.semaphore_signal(
            barrier, inc=1, device_id=(lax.rem(gz + step, gz_count), me), device_id_type=MESH
        )
        return carry

    lax.fori_loop(1, lat_count, greet_lat, 0)
    lax.fori_loop(1, gz_count, greet_gz, 0)

    zero_plane = jnp.zeros((rows, channels), BF16)
    cotp[0] = zero_plane
    cotp[lat_count + 1] = zero_plane
    orecv[0] = zero_plane
    orecv[lat_count + 1] = zero_plane

    load_cot.wait()

    def grad_plane(x, carry):
        total = ker_ref[0:1, :] * cotp[x + 2].astype(F32)
        for tap in range(1, taps):
            total = total + ker_ref[tap : tap + 1, :] * cotp[x + 2 - tap].astype(F32)
        gsend[x] = total.astype(BF16)
        return carry

    lax.fori_loop(0, lat_count, grad_plane, 0, unroll=lat_count <= 8)
    pl.semaphore_wait(barrier, lat_count + gz_count - 2)

    def grad_copy(dest):
        return pltpu.make_async_remote_copy(
            src_ref=gsend.at[dest], dst_ref=grecv.at[me], send_sem=gs_sem, recv_sem=gr_sem,
            device_id=(gz, dest), device_id_type=MESH,
        )

    def grad_start(step, carry):
        grad_copy(lax.rem(me + step, lat_count)).start()
        return carry

    lax.fori_loop(1, lat_count, grad_start, 0)
    grecv[me] = gsend[me]

    row_index = lax.broadcasted_iota(jnp.int32, (sections, sections), 0)
    col_index = lax.broadcasted_iota(jnp.int32, (sections, sections), 1)
    lower = row_index >= col_index
    step_size = step_ref[...].T
    log_decay = lax.dot_general(
        jnp.where(lower, 1.0, 0.0), -step_size * rate_ref[...], (((1,), (0,)), ((), ())),
        preferred_element_type=F32, precision=lax.Precision.HIGHEST,
    )
    middle = log_decay[sections // 2 - 1 : sections // 2]
    last = log_decay[sections - 1 : sections]
    head_index = lax.broadcasted_iota(jnp.int32, (heads, channels), 0)
    lane_index = lax.broadcasted_iota(jnp.int32, (heads, channels), 1)
    low_lane = head_index * head_size
    onehot = jnp.where(
        (lane_index >= low_lane) & (lane_index < low_lane + head_size), 1.0, 0.0
    ).astype(BF16)
    wc[...] = expand(step_size * jnp.exp(middle - log_decay), onehot)
    which = lax.broadcasted_iota(jnp.int32, (8, heads), 0)
    vectors = jnp.where(
        which == 0,
        jnp.exp(middle),
        jnp.where(which == 1, jnp.exp(last), jnp.where(which == 2, jnp.exp(last - middle), skip_ref[...])),
    )
    vecs[...] = expand(vectors, onehot)
    load_feat.wait()
    fw[...] = (wc[...] * feat[...].astype(F32)).astype(BF16)
    in_map = in_ref[...]
    out_map = out_ref[...]
    in_turned = in_map.astype(F32).T.astype(BF16)
    out_turned = out_map.astype(F32).T.astype(BF16)
    bs[...] = dot(in_turned, fw[...], 1, 0) * vecs[2:3, :]
    product = jnp.where(lower, dot(out_map, in_map, 1, 1), 0.0)
    mix = product.astype(BF16)
    mix_turned = product.T.astype(BF16)

    def forward_copy(c):
        return pltpu.make_async_remote_copy(
            src_ref=sout.at[c], dst_ref=sin.at[c], send_sem=fs_sem.at[c], recv_sem=fr_sem.at[c],
            device_id=(lax.rem(gz + 1, gz_count), me), device_id_type=MESH,
        )

    def backward_copy(c):
        return pltpu.make_async_remote_copy(
            src_ref=aout.at[c], dst_ref=ain.at[c], send_sem=bs_sem.at[c], recv_sem=br_sem.at[c],
            device_id=(lax.rem(gz + gz_count - 1, gz_count), me), device_id_type=MESH,
        )

    def out_copy(c, lanes, dest):
        return pltpu.make_async_remote_copy(
            src_ref=osend.at[dest, :, lanes], dst_ref=orecv.at[me + 1, :, lanes],
            send_sem=os_sem.at[c], recv_sem=or_sem.at[c],
            device_id=(gz, dest), device_id_type=MESH,
        )

    def span(c):
        return pl.ds(pl.multiple_of(c * width, width), width)

    def first_use():
        ec[...] = expand(jnp.exp(log_decay - middle), onehot)
        within[...] = dot(mix, fw[...], 1, 0)

    def gradients():
        pltpu.make_async_remote_copy(
            src_ref=gsend.at[pl.ds(0, lat_count - 1)], dst_ref=grecv.at[pl.ds(0, lat_count - 1)],
            send_sem=gs_sem, recv_sem=gr_sem, device_id=(gz, me), device_id_type=MESH,
        ).wait_recv()
        if aligned:
            grad[...] = grecv[...].reshape(sections, channels).astype(F32)
        else:
            for source in range(lat_count):
                grad[source * rows : (source + 1) * rows, :] = grecv[source].astype(F32)
        gr[...] = (ec[...] * grad[...]).astype(BF16)
        ad[...] = dot(out_turned, gr[...], 1, 0) * vecs[0:1, :]

    def forward_chunk(c):
        lanes = span(c)

        @pl.when(gz > 0)
        def _():
            forward_copy(c).wait_recv()

        @pl.when(gz == 0)
        def _():
            sin[c] = jnp.zeros((sin.shape[1], width), BF16)

        state = sin[c].astype(F32)

        @pl.when(gz < gz_count - 1)
        def _():
            sout[c] = (state * vecs[1:2, lanes] + bs[:, lanes]).astype(BF16)
            forward_copy(c).start()

        low = (state * vecs[0:1, lanes]).astype(BF16)
        sp[:, lanes] = low
        total = ec[:, lanes] * (within[:, lanes] + dot(out_map, low, 1, 0))
        total = total + vecs[3:4, lanes] * feat[:, lanes].astype(F32)
        if aligned:
            osend[:, :, lanes] = total.astype(BF16).reshape(lat_count, rows, width)
        else:
            wide[...] = total
            for dest in range(lat_count):
                osend[dest, :, lanes] = wide[dest * rows : (dest + 1) * rows, :].astype(BF16)

        def start(step, carry):
            out_copy(c, lanes, lax.rem(me + step, lat_count)).start()
            return carry

        lax.fori_loop(1, lat_count, start, 0)
        orecv[me + 1, :, lanes] = osend[me, :, lanes]

    def backward_chunk(c):
        lanes = span(c)

        @pl.when(gz < gz_count - 1)
        def _():
            backward_copy(c).wait_recv()

        @pl.when(gz == gz_count - 1)
        def _():
            ain[c] = jnp.zeros((ain.shape[1], width), BF16)

        state = ain[c].astype(F32)

        @pl.when(gz > 0)
        def _():
            aout[c] = (state * vecs[1:2, lanes] + ad[:, lanes]).astype(BF16)
            backward_copy(c).start()

        ap[:, lanes] = (state * vecs[2:3, lanes]).astype(BF16)

    first_use()

    def tick(step, carry):
        c = step - gz * HOP_STEPS

        @pl.when((c >= 0) & (c < chunks))
        def _():
            forward_chunk(c)

        @pl.when(step == LATE_STEPS)
        def _():
            gradients()

        e = step - LATE_STEPS - (gz_count - 1 - gz) * HOP_STEPS

        @pl.when((e >= 0) & (e < chunks))
        def _():
            backward_chunk(e)

        return carry

    lax.fori_loop(0, chunks + LATE_STEPS + (gz_count - 1) * HOP_STEPS, tick, 0)

    def plane_chunk(c, carry):
        lanes = span(c)
        pltpu.make_async_remote_copy(
            src_ref=osend.at[pl.ds(0, lat_count - 1), :, lanes],
            dst_ref=orecv.at[pl.ds(1, lat_count - 1), :, lanes],
            send_sem=os_sem.at[c], recv_sem=or_sem.at[c], device_id=(gz, me), device_id_type=MESH,
        ).wait_recv()

        def plane(x, sums):
            cot = cotp[x + 1, :, lanes].astype(F32)
            total = 0.0
            new = []
            for tap in range(taps):
                piece = orecv[x + tap, :, lanes].astype(F32)
                total = total + ker_ref[tap : tap + 1, lanes] * piece
                new.append(sums[tap] + cot * piece)
            lat_ref[x, :, lanes] = total.astype(BF16)
            return tuple(new)

        sums = lax.fori_loop(
            0, lat_count, plane, tuple(jnp.zeros((rows, width), F32) for _ in range(taps)),
            unroll=lat_count <= 8,
        )
        for tap in range(taps):
            gk1[me, tap : tap + 1, lanes] = jnp.sum(sums[tap], axis=0, keepdims=True)
        return carry

    lax.fori_loop(0, chunks, plane_chunk, 0)

    def lat_start(step, carry):
        pltpu.make_async_remote_copy(
            src_ref=gk1.at[me], dst_ref=gk1.at[me], send_sem=k_sem.at[0], recv_sem=k_sem.at[1],
            device_id=(gz, lax.rem(me + step, lat_count)), device_id_type=MESH,
        ).start()
        return carry

    lax.fori_loop(1, lat_count, lat_start, 0)

    pair = jnp.where(lower, dot(gr[...], fw[...], 1, 1), 0.0)
    gom = dot(pair.astype(BF16), in_map, 1, 0) + dot(gr[...], sp[...], 1, 1)
    gom_ref[...] = gom.astype(BF16)

    lat_all = pltpu.make_async_remote_copy(
        src_ref=gk1.at[pl.ds(0, lat_count - 1)], dst_ref=gk1.at[pl.ds(0, lat_count - 1)],
        send_sem=k_sem.at[0], recv_sem=k_sem.at[1], device_id=(gz, me), device_id_type=MESH,
    )
    lat_all.wait_recv()
    gk2[gz] = jnp.sum(gk1[...], axis=0)

    def gz_start(step, carry):
        pltpu.make_async_remote_copy(
            src_ref=gk2.at[gz], dst_ref=gk2.at[gz], send_sem=k_sem.at[2], recv_sem=k_sem.at[3],
            device_id=(lax.rem(gz + step, gz_count), me), device_id_type=MESH,
        ).start()
        return carry

    lax.fori_loop(1, gz_count, gz_start, 0)

    gim = dot(pair.T.astype(BF16), out_map, 1, 0) + dot(fw[...], ap[...], 1, 1)
    gim_ref[...] = gim.astype(BF16)
    gf = dot(mix_turned, gr[...], 1, 0) + dot(in_map, ap[...], 1, 0)
    gf_ref[...] = (wc[...] * gf + vecs[3:4, :] * grad[...]).astype(BF16)

    gz_all = pltpu.make_async_remote_copy(
        src_ref=gk2.at[pl.ds(0, gz_count - 1)], dst_ref=gk2.at[pl.ds(0, gz_count - 1)],
        send_sem=k_sem.at[2], recv_sem=k_sem.at[3], device_id=(gz, me), device_id_type=MESH,
    )
    gz_all.wait_recv()
    gk_ref[...] = jnp.sum(gk2[...], axis=0) * (1.0 / math.sqrt(row_total))

    lat_all.wait_send()
    gz_all.wait_send()
    pltpu.make_async_remote_copy(
        src_ref=gsend.at[pl.ds(0, lat_count - 1)], dst_ref=grecv.at[pl.ds(0, lat_count - 1)],
        send_sem=gs_sem, recv_sem=gr_sem, device_id=(gz, me), device_id_type=MESH,
    ).wait_send()

    def drain(c, carry):
        lanes = span(c)
        pltpu.make_async_remote_copy(
            src_ref=osend.at[pl.ds(0, lat_count - 1), :, lanes],
            dst_ref=orecv.at[pl.ds(1, lat_count - 1), :, lanes],
            send_sem=os_sem.at[c], recv_sem=or_sem.at[c], device_id=(gz, me), device_id_type=MESH,
        ).wait_send()

        @pl.when(gz < gz_count - 1)
        def _():
            forward_copy(c).wait_send()

        @pl.when(gz > 0)
        def _():
            backward_copy(c).wait_send()

        return carry

    lax.fori_loop(0, chunks, drain, 0)


def write_out(*refs):
    sources, results, sem = refs[:5], refs[5:10], refs[10]
    copies = [
        pltpu.make_async_copy(source, result, sem.at[place])
        for place, (source, result) in enumerate(zip(sources, results))
    ]
    for copy in copies:
        copy.start()
    for copy in copies:
        copy.wait()


def per_device(
    features, input_map, output_map, step_size, decay_rate, skip_gain, kernel, cotangent
):
    columns, sections, channels = features.shape
    assert columns == 1
    heads = step_size.shape[2]
    states = input_map.shape[2]
    taps = kernel.shape[0]
    assert taps == 3
    gz_count = lax.axis_size("gz")
    lat_count = lax.axis_size("lat")
    extent, rows, _ = cotangent.shape
    assert extent == lat_count
    width = 256
    chunks = channels // width
    row_total = columns * sections * gz_count * lat_count
    vmem = pl.BlockSpec(memory_space=pltpu.VMEM)
    hbm = pl.BlockSpec(memory_space=pl.ANY)
    full = (sections, channels)
    turned = (states, channels)
    held = pl.pallas_call(
        functools.partial(kernel_body, gz_count, lat_count, width, row_total),
        out_shape=(
            pltpu.VMEM(cotangent.shape, BF16),
            pltpu.VMEM(full, BF16),
            pltpu.VMEM((sections, states), BF16),
            pltpu.VMEM((sections, states), BF16),
            pltpu.VMEM((taps, channels), F32),
        ),
        in_specs=[hbm, vmem, vmem, vmem, vmem, vmem, vmem, hbm],
        out_specs=(vmem,) * 5,
        scratch_shapes=[
            pltpu.VMEM(full, BF16),
            pltpu.VMEM((extent + 2, rows, channels), BF16),
            pltpu.VMEM((lat_count, rows, channels), BF16),
            pltpu.VMEM((lat_count, rows, channels), BF16),
            pltpu.VMEM((lat_count, rows, channels), BF16),
            pltpu.VMEM((extent + 2, rows, channels), BF16),
            pltpu.VMEM((sections, width), F32),
            pltpu.VMEM(full, BF16),
            pltpu.VMEM(full, BF16),
            pltpu.VMEM(full, F32),
            pltpu.VMEM(full, F32),
            pltpu.VMEM(full, F32),
            pltpu.VMEM(full, F32),
            pltpu.VMEM(turned, F32),
            pltpu.VMEM(turned, F32),
            pltpu.VMEM((chunks, states, width), BF16),
            pltpu.VMEM((chunks, states, width), BF16),
            pltpu.VMEM((chunks, states, width), BF16),
            pltpu.VMEM((chunks, states, width), BF16),
            pltpu.VMEM(turned, BF16),
            pltpu.VMEM(turned, BF16),
            pltpu.VMEM((8, channels), F32),
            pltpu.VMEM((lat_count, taps, channels), F32),
            pltpu.VMEM((gz_count, taps, channels), F32),
            pltpu.SemaphoreType.DMA((2,)),
            pltpu.SemaphoreType.DMA,
            pltpu.SemaphoreType.DMA,
            pltpu.SemaphoreType.DMA((chunks,)),
            pltpu.SemaphoreType.DMA((chunks,)),
            pltpu.SemaphoreType.DMA((chunks,)),
            pltpu.SemaphoreType.DMA((chunks,)),
            pltpu.SemaphoreType.DMA((chunks,)),
            pltpu.SemaphoreType.DMA((chunks,)),
            pltpu.SemaphoreType.DMA((4,)),
        ],
        compiler_params=pltpu.CompilerParams(collective_id=0, has_side_effects=True),
    )(
        features,
        input_map.reshape(sections, states),
        output_map.reshape(sections, states),
        jnp.swapaxes(step_size, 1, 2).reshape(heads, sections),
        decay_rate.reshape(1, heads),
        skip_gain.reshape(1, heads),
        kernel,
        cotangent,
    )
    lateral_out, grad_features, grad_in, grad_out, grad_kernel = pl.pallas_call(
        write_out,
        out_shape=(
            jax.ShapeDtypeStruct(cotangent.shape, BF16),
            jax.ShapeDtypeStruct(full, BF16),
            jax.ShapeDtypeStruct((sections, states), BF16),
            jax.ShapeDtypeStruct((sections, states), BF16),
            jax.ShapeDtypeStruct((taps, channels), F32),
        ),
        in_specs=[vmem] * 5,
        out_specs=(hbm,) * 5,
        scratch_shapes=[pltpu.SemaphoreType.DMA((5,))],
    )(*(pltpu.with_memory_space_constraint(one, pltpu.VMEM) for one in held))
    return (
        lateral_out,
        grad_features.reshape(features.shape),
        grad_in.reshape(input_map.shape),
        grad_out.reshape(output_map.shape),
        grad_kernel,
    )


def solution(mesh):
    in_specs = (
        P("lat", "gz", None),
        P("lat", "gz", None),
        P("lat", "gz", None),
        P("lat", "gz", None),
        P(),
        P(),
        P(),
        P(None, ("gz", "lat"), None),
    )
    out_specs = (
        P(None, ("gz", "lat"), None),
        P("lat", "gz", None),
        P("lat", "gz", None),
        P("lat", "gz", None),
        P(),
    )
    return jax.shard_map(
        per_device, mesh=mesh, in_specs=in_specs, out_specs=out_specs, check_vma=False
    )
```

```python
import functools
import math

import jax
import jax.numpy as jnp
from jax import lax
from jax.experimental import pallas as pl
from jax.experimental.pallas import tpu as pltpu
from jax.sharding import PartitionSpec as P

F32 = jnp.float32
BF16 = jnp.bfloat16
MESH = pl.DeviceIdType.MESH
HOP_STEPS = 2
LATE_STEPS = 4
PLANE_STEPS = 3
SUM_STEPS = 2


def dot(a, b, da, db):
    return lax.dot_general(a, b, (((da,), (db,)), ((), ())), preferred_element_type=F32)


def expand(values, onehot):
    high = values.astype(BF16)
    low = (values - high.astype(F32)).astype(BF16)
    return dot(high, onehot, 1, 0) + dot(low, onehot, 1, 0)


def kernel_body(
    gz_count, lat_count, width, row_total,
    feat_hbm, in_hbm, out_hbm, step_hbm, rate_hbm, skip_hbm, ker_hbm, cot_hbm,
    lat_ref, gf_ref, gim_ref, gom_ref, gk_ref,
    feat, cotp, gsend, grecv, osend, orecv, wide,
    fw, gr, grad, ec, wc, within, bs, ad, sin, sout, ain, aout, sp, ap, vecs, gk1, gk2, pair_turned,
    in_ref, out_ref, step_ref, rate_ref, skip_ref, ker_ref,
    load_sem, gs_sem, gr_sem, os_sem, or_sem, fs_sem, fr_sem, bs_sem, br_sem, k_sem,
):
    gz = lax.axis_index("gz")
    me = lax.axis_index("lat")
    sections, channels = feat.shape
    heads = step_ref.shape[0]
    head_size = channels // heads
    rows = gsend.shape[1]
    taps = ker_ref.shape[0]
    chunks = channels // width
    aligned = rows % 16 == 0

    load_cot = pltpu.make_async_copy(cot_hbm, cotp.at[pl.ds(1, lat_count)], load_sem.at[0])
    load_feat = pltpu.make_async_copy(feat_hbm.at[0], feat, load_sem.at[1])
    small = [
        pltpu.make_async_copy(source, target, load_sem.at[2 + place])
        for place, (source, target) in enumerate(
            (
                (step_hbm, step_ref),
                (rate_hbm, rate_ref),
                (skip_hbm, skip_ref),
                (ker_hbm, ker_ref),
                (in_hbm, in_ref),
                (out_hbm, out_ref),
            )
        )
    ]
    for copy in small[:4]:
        copy.start()
    load_cot.start()
    small[4].start()
    load_feat.start()
    small[5].start()

    barrier = pltpu.get_barrier_semaphore()

    def greet_lat(step, carry):
        pl.semaphore_signal(
            barrier, inc=1, device_id=(gz, lax.rem(me + step, lat_count)), device_id_type=MESH
        )
        return carry

    def greet_gz(step, carry):
        pl.semaphore_signal(
            barrier, inc=1, device_id=(lax.rem(gz + step, gz_count), me), device_id_type=MESH
        )
        return carry

    lax.fori_loop(1, lat_count, greet_lat, 0)
    lax.fori_loop(1, gz_count, greet_gz, 0)

    zero_plane = jnp.zeros((rows, channels), BF16)
    cotp[0] = zero_plane
    cotp[lat_count + 1] = zero_plane
    orecv[0] = zero_plane
    orecv[lat_count + 1] = zero_plane

    for copy in small[:4]:
        copy.wait()
    row_index = lax.broadcasted_iota(jnp.int32, (sections, sections), 0)
    col_index = lax.broadcasted_iota(jnp.int32, (sections, sections), 1)
    lower = row_index >= col_index
    step_size = step_ref[...].T
    log_decay = lax.dot_general(
        jnp.where(lower, 1.0, 0.0), -step_size * rate_ref[...], (((1,), (0,)), ((), ())),
        preferred_element_type=F32, precision=lax.Precision.HIGHEST,
    )
    middle = log_decay[sections // 2 - 1 : sections // 2]
    last = log_decay[sections - 1 : sections]
    head_index = lax.broadcasted_iota(jnp.int32, (heads, channels), 0)
    lane_index = lax.broadcasted_iota(jnp.int32, (heads, channels), 1)
    low_lane = head_index * head_size
    onehot = jnp.where(
        (lane_index >= low_lane) & (lane_index < low_lane + head_size), 1.0, 0.0
    ).astype(BF16)
    wc[...] = expand(step_size * jnp.exp(middle - log_decay), onehot)
    which = lax.broadcasted_iota(jnp.int32, (8, heads), 0)
    vectors = jnp.where(
        which == 0,
        jnp.exp(middle),
        jnp.where(which == 1, jnp.exp(last), jnp.where(which == 2, jnp.exp(last - middle), skip_ref[...])),
    )
    vecs[...] = expand(vectors, onehot)
    ec[...] = expand(jnp.exp(log_decay - middle), onehot)

    load_cot.wait()

    def grad_plane(x, carry):
        total = ker_ref[0:1, :] * cotp[x + 2].astype(F32)
        for tap in range(1, taps):
            total = total + ker_ref[tap : tap + 1, :] * cotp[x + 2 - tap].astype(F32)
        gsend[x] = total.astype(BF16)
        return carry

    lax.fori_loop(0, lat_count, grad_plane, 0, unroll=lat_count <= 8)
    pl.semaphore_wait(barrier, lat_count + gz_count - 2)

    def grad_copy(dest):
        return pltpu.make_async_remote_copy(
            src_ref=gsend.at[dest], dst_ref=grecv.at[me], send_sem=gs_sem, recv_sem=gr_sem,
            device_id=(gz, dest), device_id_type=MESH,
        )

    def grad_start(step, carry):
        grad_copy(lax.rem(me + step, lat_count)).start()
        return carry

    lax.fori_loop(1, lat_count, grad_start, 0)
    grecv[me] = gsend[me]

    load_feat.wait()
    small[4].wait()
    small[5].wait()
    fw[...] = (wc[...] * feat[...].astype(F32)).astype(BF16)
    in_map = in_ref[...]
    out_map = out_ref[...]
    in_turned = in_map.astype(F32).T.astype(BF16)
    out_turned = out_map.astype(F32).T.astype(BF16)
    bs[...] = dot(in_turned, fw[...], 1, 0) * vecs[2:3, :]

    def forward_copy(c):
        return pltpu.make_async_remote_copy(
            src_ref=sout.at[c], dst_ref=sin.at[c], send_sem=fs_sem.at[c], recv_sem=fr_sem.at[c],
            device_id=(lax.rem(gz + 1, gz_count), me), device_id_type=MESH,
        )

    def backward_copy(c):
        return pltpu.make_async_remote_copy(
            src_ref=aout.at[c], dst_ref=ain.at[c], send_sem=bs_sem.at[c], recv_sem=br_sem.at[c],
            device_id=(lax.rem(gz + gz_count - 1, gz_count), me), device_id_type=MESH,
        )

    def out_copy(c, lanes, dest):
        return pltpu.make_async_remote_copy(
            src_ref=osend.at[dest, :, lanes], dst_ref=orecv.at[me + 1, :, lanes],
            send_sem=os_sem.at[c], recv_sem=or_sem.at[c],
            device_id=(gz, dest), device_id_type=MESH,
        )

    def span(c):
        return pl.ds(pl.multiple_of(c * width, width), width)

    def gradients():
        pltpu.make_async_remote_copy(
            src_ref=gsend.at[pl.ds(0, lat_count - 1)], dst_ref=grecv.at[pl.ds(0, lat_count - 1)],
            send_sem=gs_sem, recv_sem=gr_sem, device_id=(gz, me), device_id_type=MESH,
        ).wait_recv()
        if aligned:
            grad[...] = grecv[...].reshape(sections, channels).astype(F32)
        else:
            for source in range(lat_count):
                grad[source * rows : (source + 1) * rows, :] = grecv[source].astype(F32)
        gr[...] = (ec[...] * grad[...]).astype(BF16)
        ad[...] = dot(out_turned, gr[...], 1, 0) * vecs[0:1, :]

        @pl.when(gz == gz_count - 1)
        def _():
            def send(c, carry):
                aout[c] = ad[:, span(c)].astype(BF16)
                backward_copy(c).start()
                return carry

            lax.fori_loop(0, chunks, send, 0)

    def forward_chunk(c):
        lanes = span(c)

        @pl.when(gz > 0)
        def _():
            forward_copy(c).wait_recv()

        @pl.when(gz == 0)
        def _():
            sin[c] = jnp.zeros((sin.shape[1], width), BF16)

        state = sin[c].astype(F32)

        @pl.when((gz > 0) & (gz < gz_count - 1))
        def _():
            sout[c] = (state * vecs[1:2, lanes] + bs[:, lanes]).astype(BF16)
            forward_copy(c).start()

        low = (state * vecs[0:1, lanes]).astype(BF16)
        sp[:, lanes] = low
        total = ec[:, lanes] * (within[:, lanes] + dot(out_map, low, 1, 0))
        total = total + vecs[3:4, lanes] * feat[:, lanes].astype(F32)
        if aligned:
            osend[:, :, lanes] = total.astype(BF16).reshape(lat_count, rows, width)
        else:
            wide[...] = total
            for dest in range(lat_count):
                osend[dest, :, lanes] = wide[dest * rows : (dest + 1) * rows, :].astype(BF16)

        def start(step, carry):
            out_copy(c, lanes, lax.rem(me + step, lat_count)).start()
            return carry

        lax.fori_loop(1, lat_count, start, 0)
        orecv[me + 1, :, lanes] = osend[me, :, lanes]

    def backward_chunk(c):
        lanes = span(c)

        @pl.when(gz < gz_count - 1)
        def _():
            backward_copy(c).wait_recv()

        @pl.when(gz == gz_count - 1)
        def _():
            ain[c] = jnp.zeros((ain.shape[1], width), BF16)

        state = ain[c].astype(F32)

        @pl.when((gz > 0) & (gz < gz_count - 1))
        def _():
            aout[c] = (state * vecs[1:2, lanes] + ad[:, lanes]).astype(BF16)
            backward_copy(c).start()

        ap[:, lanes] = (state * vecs[2:3, lanes]).astype(BF16)

    @pl.when(gz == 0)
    def _():
        def send(c, carry):
            sout[c] = bs[:, span(c)].astype(BF16)
            forward_copy(c).start()
            return carry

        lax.fori_loop(0, chunks, send, 0)

    product = jnp.where(lower, dot(out_map, in_map, 1, 1), 0.0)
    mix = product.astype(BF16)
    mix_turned = product.T.astype(BF16)
    within[...] = dot(mix, fw[...], 1, 0)

    def plane_chunk(c):
        lanes = span(c)
        pltpu.make_async_remote_copy(
            src_ref=osend.at[pl.ds(0, lat_count - 1), :, lanes],
            dst_ref=orecv.at[pl.ds(1, lat_count - 1), :, lanes],
            send_sem=os_sem.at[c], recv_sem=or_sem.at[c], device_id=(gz, me), device_id_type=MESH,
        ).wait_recv()

        def plane(x, sums):
            cot = cotp[x + 1, :, lanes].astype(F32)
            total = 0.0
            new = []
            for tap in range(taps):
                piece = orecv[x + tap, :, lanes].astype(F32)
                total = total + ker_ref[tap : tap + 1, lanes] * piece
                new.append(sums[tap] + cot * piece)
            lat_ref[x, :, lanes] = total.astype(BF16)
            return tuple(new)

        sums = lax.fori_loop(
            0, lat_count, plane, tuple(jnp.zeros((rows, width), F32) for _ in range(taps)),
            unroll=lat_count <= 8,
        )
        for tap in range(taps):
            row = jnp.sum(sums[tap], axis=0, keepdims=True)
            for tile in range(width // 128):
                place = tap * (channels // 128) + c * (width // 128) + tile
                gk1[me, pl.ds(place, 1), :] = row[:, tile * 128 : (tile + 1) * 128]


    def lat_start(step, carry):
        pltpu.make_async_remote_copy(
            src_ref=gk1.at[me], dst_ref=gk1.at[me], send_sem=k_sem.at[0], recv_sem=k_sem.at[1],
            device_id=(gz, lax.rem(me + step, lat_count)), device_id_type=MESH,
        ).start()
        return carry

    lat_all = pltpu.make_async_remote_copy(
        src_ref=gk1.at[pl.ds(0, lat_count - 1)], dst_ref=gk1.at[pl.ds(0, lat_count - 1)],
        send_sem=k_sem.at[0], recv_sem=k_sem.at[1], device_id=(gz, me), device_id_type=MESH,
    )
    def gz_start(step, carry):
        pltpu.make_async_remote_copy(
            src_ref=gk2.at[gz], dst_ref=gk2.at[gz], send_sem=k_sem.at[2], recv_sem=k_sem.at[3],
            device_id=(lax.rem(gz + step, gz_count), me), device_id_type=MESH,
        ).start()
        return carry

    def lat_begin():
        lax.fori_loop(1, lat_count, lat_start, 0)
        pair = jnp.where(lower, dot(gr[...], fw[...], 1, 1), 0.0)
        gom = dot(pair.astype(BF16), in_map, 1, 0) + dot(gr[...], sp[...], 1, 1)
        gom_ref[...] = gom.astype(BF16)
        pair_turned[...] = pair.T.astype(BF16)

    def lat_end():
        lat_all.wait_recv()
        gk2[gz] = jnp.sum(gk1[...], axis=0)

        lax.fori_loop(1, gz_count, gz_start, 0)

    def tick(step, carry):
        c = step - gz * HOP_STEPS

        @pl.when((c >= 0) & (c < chunks))
        def _():
            forward_chunk(c)

        e = step - LATE_STEPS - (gz_count - 1 - gz) * HOP_STEPS

        @pl.when(step == LATE_STEPS)
        def _():
            gradients()

        @pl.when((e >= 0) & (e < chunks))
        def _():
            backward_chunk(e)

        f = c - PLANE_STEPS

        @pl.when((f >= 0) & (f < chunks))
        def _():
            plane_chunk(f)

        @pl.when(f == chunks)
        def _():
            lat_begin()

        @pl.when(f == chunks + SUM_STEPS)
        def _():
            lat_end()

        return carry

    ticks = chunks + (gz_count - 1) * HOP_STEPS + max(LATE_STEPS, PLANE_STEPS + SUM_STEPS + 1)
    lax.fori_loop(0, ticks, tick, 0)

    gim = dot(pair_turned[...], out_map, 1, 0) + dot(fw[...], ap[...], 1, 1)
    gim_ref[...] = gim.astype(BF16)
    gf = dot(mix_turned, gr[...], 1, 0) + dot(in_map, ap[...], 1, 0)
    gf_ref[...] = (wc[...] * gf + vecs[3:4, :] * grad[...]).astype(BF16)

    gz_all = pltpu.make_async_remote_copy(
        src_ref=gk2.at[pl.ds(0, gz_count - 1)], dst_ref=gk2.at[pl.ds(0, gz_count - 1)],
        send_sem=k_sem.at[2], recv_sem=k_sem.at[3], device_id=(gz, me), device_id_type=MESH,
    )
    gz_all.wait_recv()
    packed = jnp.sum(gk2[...], axis=0) * (1.0 / math.sqrt(row_total))
    for tap in range(taps):
        for tile in range(channels // 128):
            place = tap * (channels // 128) + tile
            gk_ref[tap : tap + 1, tile * 128 : (tile + 1) * 128] = packed[place : place + 1, :]

    lat_all.wait_send()
    gz_all.wait_send()
    pltpu.make_async_remote_copy(
        src_ref=gsend.at[pl.ds(0, lat_count - 1)], dst_ref=grecv.at[pl.ds(0, lat_count - 1)],
        send_sem=gs_sem, recv_sem=gr_sem, device_id=(gz, me), device_id_type=MESH,
    ).wait_send()

    def drain(c, carry):
        lanes = span(c)
        pltpu.make_async_remote_copy(
            src_ref=osend.at[pl.ds(0, lat_count - 1), :, lanes],
            dst_ref=orecv.at[pl.ds(1, lat_count - 1), :, lanes],
            send_sem=os_sem.at[c], recv_sem=or_sem.at[c], device_id=(gz, me), device_id_type=MESH,
        ).wait_send()

        @pl.when(gz < gz_count - 1)
        def _():
            forward_copy(c).wait_send()

        @pl.when(gz > 0)
        def _():
            backward_copy(c).wait_send()

        return carry

    lax.fori_loop(0, chunks, drain, 0)


def write_out(*refs):
    sources, results, sem = refs[:5], refs[5:10], refs[10]
    copies = [
        pltpu.make_async_copy(source, result, sem.at[place])
        for place, (source, result) in enumerate(zip(sources, results))
    ]
    for copy in copies:
        copy.start()
    for copy in copies:
        copy.wait()


def per_device(
    features, input_map, output_map, step_size, decay_rate, skip_gain, kernel, cotangent
):
    columns, sections, channels = features.shape
    assert columns == 1
    heads = step_size.shape[2]
    states = input_map.shape[2]
    taps = kernel.shape[0]
    assert taps == 3
    gz_count = lax.axis_size("gz")
    lat_count = lax.axis_size("lat")
    extent, rows, _ = cotangent.shape
    assert extent == lat_count
    width = 256
    chunks = channels // width
    row_total = columns * sections * gz_count * lat_count
    vmem = pl.BlockSpec(memory_space=pltpu.VMEM)
    hbm = pl.BlockSpec(memory_space=pl.ANY)
    full = (sections, channels)
    turned = (states, channels)
    held = pl.pallas_call(
        functools.partial(kernel_body, gz_count, lat_count, width, row_total),
        out_shape=(
            pltpu.VMEM(cotangent.shape, BF16),
            pltpu.VMEM(full, BF16),
            pltpu.VMEM((sections, states), BF16),
            pltpu.VMEM((sections, states), BF16),
            pltpu.VMEM((taps, channels), F32),
        ),
        in_specs=[hbm] * 8,
        out_specs=(vmem,) * 5,
        scratch_shapes=[
            pltpu.VMEM(full, BF16),
            pltpu.VMEM((extent + 2, rows, channels), BF16),
            pltpu.VMEM((lat_count, rows, channels), BF16),
            pltpu.VMEM((lat_count, rows, channels), BF16),
            pltpu.VMEM((lat_count, rows, channels), BF16),
            pltpu.VMEM((extent + 2, rows, channels), BF16),
            pltpu.VMEM((sections, width), F32),
            pltpu.VMEM(full, BF16),
            pltpu.VMEM(full, BF16),
            pltpu.VMEM(full, F32),
            pltpu.VMEM(full, F32),
            pltpu.VMEM(full, F32),
            pltpu.VMEM(full, F32),
            pltpu.VMEM(turned, F32),
            pltpu.VMEM(turned, F32),
            pltpu.VMEM((chunks, states, width), BF16),
            pltpu.VMEM((chunks, states, width), BF16),
            pltpu.VMEM((chunks, states, width), BF16),
            pltpu.VMEM((chunks, states, width), BF16),
            pltpu.VMEM(turned, BF16),
            pltpu.VMEM(turned, BF16),
            pltpu.VMEM((8, channels), F32),
            pltpu.VMEM((lat_count, taps * channels // 128, 128), F32),
            pltpu.VMEM((gz_count, taps * channels // 128, 128), F32),
            pltpu.VMEM((sections, sections), BF16),
            pltpu.VMEM((sections, states), BF16),
            pltpu.VMEM((sections, states), BF16),
            pltpu.VMEM((heads, sections), F32),
            pltpu.VMEM((1, heads), F32),
            pltpu.VMEM((1, heads), F32),
            pltpu.VMEM((taps, channels), F32),
            pltpu.SemaphoreType.DMA((8,)),
            pltpu.SemaphoreType.DMA,
            pltpu.SemaphoreType.DMA,
            pltpu.SemaphoreType.DMA((chunks,)),
            pltpu.SemaphoreType.DMA((chunks,)),
            pltpu.SemaphoreType.DMA((chunks,)),
            pltpu.SemaphoreType.DMA((chunks,)),
            pltpu.SemaphoreType.DMA((chunks,)),
            pltpu.SemaphoreType.DMA((chunks,)),
            pltpu.SemaphoreType.DMA((4,)),
        ],
        compiler_params=pltpu.CompilerParams(collective_id=0, has_side_effects=True),
    )(
        features,
        input_map.reshape(sections, states),
        output_map.reshape(sections, states),
        jnp.swapaxes(step_size, 1, 2).reshape(heads, sections),
        decay_rate.reshape(1, heads),
        skip_gain.reshape(1, heads),
        kernel,
        cotangent,
    )
    lateral_out, grad_features, grad_in, grad_out, grad_kernel = pl.pallas_call(
        write_out,
        out_shape=(
            jax.ShapeDtypeStruct(cotangent.shape, BF16),
            jax.ShapeDtypeStruct(full, BF16),
            jax.ShapeDtypeStruct((sections, states), BF16),
            jax.ShapeDtypeStruct((sections, states), BF16),
            jax.ShapeDtypeStruct((taps, channels), F32),
        ),
        in_specs=[vmem] * 5,
        out_specs=(hbm,) * 5,
        scratch_shapes=[pltpu.SemaphoreType.DMA((5,))],
    )(*(pltpu.with_memory_space_constraint(one, pltpu.VMEM) for one in held))
    return (
        lateral_out,
        grad_features.reshape(features.shape),
        grad_in.reshape(input_map.shape),
        grad_out.reshape(output_map.shape),
        grad_kernel,
    )


def solution(mesh):
    in_specs = (
        P("lat", "gz", None),
        P("lat", "gz", None),
        P("lat", "gz", None),
        P("lat", "gz", None),
        P(),
        P(),
        P(),
        P(None, ("gz", "lat"), None),
    )
    out_specs = (
        P(None, ("gz", "lat"), None),
        P("lat", "gz", None),
        P("lat", "gz", None),
        P("lat", "gz", None),
        P(),
    )
    return jax.shard_map(
        per_device, mesh=mesh, in_specs=in_specs, out_specs=out_specs, check_vma=False
    )
```

```python
import functools
import math

import jax
import jax.numpy as jnp
from jax import lax
from jax.experimental import pallas as pl
from jax.experimental.pallas import tpu as pltpu
from jax.sharding import PartitionSpec as P

F32 = jnp.float32
BF16 = jnp.bfloat16
MESH = pl.DeviceIdType.MESH
HOP_STEPS = 2
LATE_STEPS = 4
PLANE_STEPS = 3
SUM_STEPS = 2


def dot(a, b, da, db):
    return lax.dot_general(a, b, (((da,), (db,)), ((), ())), preferred_element_type=F32)


def expand(values, onehot):
    high = values.astype(BF16)
    low = (values - high.astype(F32)).astype(BF16)
    return dot(high, onehot, 1, 0) + dot(low, onehot, 1, 0)


def kernel_body(
    gz_count, lat_count, width, row_total,
    feat_hbm, in_hbm, out_hbm, step_hbm, rate_hbm, skip_hbm, ker_hbm, cot_hbm,
    lat_ref, gf_ref, gim_ref, gom_ref, gk_ref,
    feat, cotp, gsend, grecv, osend, orecv, wide,
    fw, gr, grad, ec, wc, within, bs, ad, sin, sout, ain, aout, sp, ap, vecs, gk1, gk2, pair_turned,
    in_ref, out_ref, step_ref, rate_ref, skip_ref, ker_ref,
    load_sem, gs_sem, gr_sem, os_sem, or_sem, fs_sem, fr_sem, bs_sem, br_sem, k_sem,
):
    gz = lax.axis_index("gz")
    me = lax.axis_index("lat")
    sections, channels = feat.shape
    heads = step_ref.shape[0]
    head_size = channels // heads
    rows = gsend.shape[1]
    taps = ker_ref.shape[0]
    chunks = channels // width
    half = chunks // 2
    part = half * width // 128
    aligned = rows % 16 == 0

    load_cot = pltpu.make_async_copy(cot_hbm, cotp.at[pl.ds(1, lat_count)], load_sem.at[0])
    load_feat = pltpu.make_async_copy(feat_hbm.at[0], feat, load_sem.at[1])
    small = [
        pltpu.make_async_copy(source, target, load_sem.at[2 + place])
        for place, (source, target) in enumerate(
            (
                (step_hbm, step_ref),
                (rate_hbm, rate_ref),
                (skip_hbm, skip_ref),
                (ker_hbm, ker_ref),
                (in_hbm, in_ref),
                (out_hbm, out_ref),
            )
        )
    ]
    for copy in small[:4]:
        copy.start()
    load_cot.start()
    small[4].start()
    load_feat.start()
    small[5].start()

    barrier = pltpu.get_barrier_semaphore()

    def greet_lat(step, carry):
        pl.semaphore_signal(
            barrier, inc=1, device_id=(gz, lax.rem(me + step, lat_count)), device_id_type=MESH
        )
        return carry

    def greet_gz(step, carry):
        pl.semaphore_signal(
            barrier, inc=1, device_id=(lax.rem(gz + step, gz_count), me), device_id_type=MESH
        )
        return carry

    lax.fori_loop(1, lat_count, greet_lat, 0)
    lax.fori_loop(1, gz_count, greet_gz, 0)

    zero_plane = jnp.zeros((rows, channels), BF16)
    cotp[0] = zero_plane
    cotp[lat_count + 1] = zero_plane
    orecv[0] = zero_plane
    orecv[lat_count + 1] = zero_plane

    for copy in small[:4]:
        copy.wait()
    row_index = lax.broadcasted_iota(jnp.int32, (sections, sections), 0)
    col_index = lax.broadcasted_iota(jnp.int32, (sections, sections), 1)
    lower = row_index >= col_index
    step_size = step_ref[...].T
    log_decay = lax.dot_general(
        jnp.where(lower, 1.0, 0.0), -step_size * rate_ref[...], (((1,), (0,)), ((), ())),
        preferred_element_type=F32, precision=lax.Precision.HIGHEST,
    )
    middle = log_decay[sections // 2 - 1 : sections // 2]
    last = log_decay[sections - 1 : sections]
    head_index = lax.broadcasted_iota(jnp.int32, (heads, channels), 0)
    lane_index = lax.broadcasted_iota(jnp.int32, (heads, channels), 1)
    low_lane = head_index * head_size
    onehot = jnp.where(
        (lane_index >= low_lane) & (lane_index < low_lane + head_size), 1.0, 0.0
    ).astype(BF16)
    wc[...] = expand(step_size * jnp.exp(middle - log_decay), onehot)
    which = lax.broadcasted_iota(jnp.int32, (8, heads), 0)
    vectors = jnp.where(
        which == 0,
        jnp.exp(middle),
        jnp.where(which == 1, jnp.exp(last), jnp.where(which == 2, jnp.exp(last - middle), skip_ref[...])),
    )
    vecs[...] = expand(vectors, onehot)
    ec[...] = expand(jnp.exp(log_decay - middle), onehot)

    load_cot.wait()

    def grad_plane(x, carry):
        total = ker_ref[0:1, :] * cotp[x + 2].astype(F32)
        for tap in range(1, taps):
            total = total + ker_ref[tap : tap + 1, :] * cotp[x + 2 - tap].astype(F32)
        gsend[x] = total.astype(BF16)
        return carry

    lax.fori_loop(0, lat_count, grad_plane, 0, unroll=lat_count <= 8)
    pl.semaphore_wait(barrier, lat_count + gz_count - 2)

    def grad_copy(dest):
        return pltpu.make_async_remote_copy(
            src_ref=gsend.at[dest], dst_ref=grecv.at[me], send_sem=gs_sem, recv_sem=gr_sem,
            device_id=(gz, dest), device_id_type=MESH,
        )

    def grad_start(step, carry):
        grad_copy(lax.rem(me + step, lat_count)).start()
        return carry

    lax.fori_loop(1, lat_count, grad_start, 0)
    grecv[me] = gsend[me]

    load_feat.wait()
    small[4].wait()
    small[5].wait()
    fw[...] = (wc[...] * feat[...].astype(F32)).astype(BF16)
    in_map = in_ref[...]
    out_map = out_ref[...]
    in_turned = in_map.astype(F32).T.astype(BF16)
    out_turned = out_map.astype(F32).T.astype(BF16)
    bs[...] = dot(in_turned, fw[...], 1, 0) * vecs[2:3, :]

    def forward_copy(c):
        return pltpu.make_async_remote_copy(
            src_ref=sout.at[c], dst_ref=sin.at[c], send_sem=fs_sem.at[c], recv_sem=fr_sem.at[c],
            device_id=(lax.rem(gz + 1, gz_count), me), device_id_type=MESH,
        )

    def backward_copy(c):
        return pltpu.make_async_remote_copy(
            src_ref=aout.at[c], dst_ref=ain.at[c], send_sem=bs_sem.at[c], recv_sem=br_sem.at[c],
            device_id=(lax.rem(gz + gz_count - 1, gz_count), me), device_id_type=MESH,
        )

    def out_copy(c, lanes, dest):
        return pltpu.make_async_remote_copy(
            src_ref=osend.at[dest, :, lanes], dst_ref=orecv.at[me + 1, :, lanes],
            send_sem=os_sem.at[c], recv_sem=or_sem.at[c],
            device_id=(gz, dest), device_id_type=MESH,
        )

    def span(c):
        return pl.ds(pl.multiple_of(c * width, width), width)

    def gradients():
        pltpu.make_async_remote_copy(
            src_ref=gsend.at[pl.ds(0, lat_count - 1)], dst_ref=grecv.at[pl.ds(0, lat_count - 1)],
            send_sem=gs_sem, recv_sem=gr_sem, device_id=(gz, me), device_id_type=MESH,
        ).wait_recv()
        if aligned:
            grad[...] = grecv[...].reshape(sections, channels).astype(F32)
        else:
            for source in range(lat_count):
                grad[source * rows : (source + 1) * rows, :] = grecv[source].astype(F32)
        gr[...] = (ec[...] * grad[...]).astype(BF16)
        ad[...] = dot(out_turned, gr[...], 1, 0) * vecs[0:1, :]

        @pl.when(gz == gz_count - 1)
        def _():
            def send(c, carry):
                aout[c] = ad[:, span(c)].astype(BF16)
                backward_copy(c).start()
                return carry

            lax.fori_loop(0, chunks, send, 0)

    def forward_chunk(c):
        lanes = span(c)

        @pl.when(gz > 0)
        def _():
            forward_copy(c).wait_recv()

        @pl.when(gz == 0)
        def _():
            sin[c] = jnp.zeros((sin.shape[1], width), BF16)

        state = sin[c].astype(F32)

        @pl.when((gz > 0) & (gz < gz_count - 1))
        def _():
            sout[c] = (state * vecs[1:2, lanes] + bs[:, lanes]).astype(BF16)
            forward_copy(c).start()

        low = (state * vecs[0:1, lanes]).astype(BF16)
        sp[:, lanes] = low
        total = ec[:, lanes] * (within[:, lanes] + dot(out_map, low, 1, 0))
        total = total + vecs[3:4, lanes] * feat[:, lanes].astype(F32)
        if aligned:
            osend[:, :, lanes] = total.astype(BF16).reshape(lat_count, rows, width)
        else:
            wide[...] = total
            for dest in range(lat_count):
                osend[dest, :, lanes] = wide[dest * rows : (dest + 1) * rows, :].astype(BF16)

        def start(step, carry):
            out_copy(c, lanes, lax.rem(me + step, lat_count)).start()
            return carry

        lax.fori_loop(1, lat_count, start, 0)
        orecv[me + 1, :, lanes] = osend[me, :, lanes]

    def backward_chunk(c):
        lanes = span(c)

        @pl.when(gz < gz_count - 1)
        def _():
            backward_copy(c).wait_recv()

        @pl.when(gz == gz_count - 1)
        def _():
            ain[c] = jnp.zeros((ain.shape[1], width), BF16)

        state = ain[c].astype(F32)

        @pl.when((gz > 0) & (gz < gz_count - 1))
        def _():
            aout[c] = (state * vecs[1:2, lanes] + ad[:, lanes]).astype(BF16)
            backward_copy(c).start()

        ap[:, lanes] = (state * vecs[2:3, lanes]).astype(BF16)

    @pl.when(gz == 0)
    def _():
        def send(c, carry):
            sout[c] = bs[:, span(c)].astype(BF16)
            forward_copy(c).start()
            return carry

        lax.fori_loop(0, chunks, send, 0)

    product = jnp.where(lower, dot(out_map, in_map, 1, 1), 0.0)
    mix = product.astype(BF16)
    mix_turned = product.T.astype(BF16)
    within[...] = dot(mix, fw[...], 1, 0)

    def plane_chunk(c):
        lanes = span(c)
        pltpu.make_async_remote_copy(
            src_ref=osend.at[pl.ds(0, lat_count - 1), :, lanes],
            dst_ref=orecv.at[pl.ds(1, lat_count - 1), :, lanes],
            send_sem=os_sem.at[c], recv_sem=or_sem.at[c], device_id=(gz, me), device_id_type=MESH,
        ).wait_recv()

        def plane(x, sums):
            cot = cotp[x + 1, :, lanes].astype(F32)
            total = 0.0
            new = []
            for tap in range(taps):
                piece = orecv[x + tap, :, lanes].astype(F32)
                total = total + ker_ref[tap : tap + 1, lanes] * piece
                new.append(sums[tap] + cot * piece)
            lat_ref[x, :, lanes] = total.astype(BF16)
            return tuple(new)

        sums = lax.fori_loop(
            0, lat_count, plane, tuple(jnp.zeros((rows, width), F32) for _ in range(taps)),
            unroll=lat_count <= 8,
        )
        for tap in range(taps):
            row = jnp.sum(sums[tap], axis=0, keepdims=True)
            for tile in range(width // 128):
                place = tap * part + lax.rem(c, half) * (width // 128) + tile
                gk1[c // half, me, pl.ds(place, 1), :] = row[:, tile * 128 : (tile + 1) * 128]


    def lat_start(group, dest):
        return pltpu.make_async_remote_copy(
            src_ref=gk1.at[group, me], dst_ref=gk1.at[group, me],
            send_sem=k_sem.at[4 * group], recv_sem=k_sem.at[4 * group + 1],
            device_id=(gz, dest), device_id_type=MESH,
        )

    def lat_all(group):
        return pltpu.make_async_remote_copy(
            src_ref=gk1.at[group, pl.ds(0, lat_count - 1)],
            dst_ref=gk1.at[group, pl.ds(0, lat_count - 1)],
            send_sem=k_sem.at[4 * group], recv_sem=k_sem.at[4 * group + 1],
            device_id=(gz, me), device_id_type=MESH,
        )

    def gz_start(group, dest):
        return pltpu.make_async_remote_copy(
            src_ref=gk2.at[group, gz], dst_ref=gk2.at[group, gz],
            send_sem=k_sem.at[4 * group + 2], recv_sem=k_sem.at[4 * group + 3],
            device_id=(dest, me), device_id_type=MESH,
        )

    def gz_all(group):
        return pltpu.make_async_remote_copy(
            src_ref=gk2.at[group, pl.ds(0, gz_count - 1)],
            dst_ref=gk2.at[group, pl.ds(0, gz_count - 1)],
            send_sem=k_sem.at[4 * group + 2], recv_sem=k_sem.at[4 * group + 3],
            device_id=(gz, me), device_id_type=MESH,
        )

    def lat_begin(group):
        def send(step, carry):
            lat_start(group, lax.rem(me + step, lat_count)).start()
            return carry

        lax.fori_loop(1, lat_count, send, 0)

    def lat_end(group):
        lat_all(group).wait_recv()
        gk2[group, gz] = jnp.sum(gk1[group], axis=0)

        def send(step, carry):
            gz_start(group, lax.rem(gz + step, gz_count)).start()
            return carry

        lax.fori_loop(1, gz_count, send, 0)

    def pairs():
        pair = jnp.where(lower, dot(gr[...], fw[...], 1, 1), 0.0)
        gom = dot(pair.astype(BF16), in_map, 1, 0) + dot(gr[...], sp[...], 1, 1)
        gom_ref[...] = gom.astype(BF16)
        pair_turned[...] = pair.T.astype(BF16)

    def tick(step, carry):
        c = step - gz * HOP_STEPS

        @pl.when((c >= 0) & (c < chunks))
        def _():
            forward_chunk(c)

        e = step - LATE_STEPS - (gz_count - 1 - gz) * HOP_STEPS

        @pl.when(step == LATE_STEPS)
        def _():
            gradients()

        @pl.when((e >= 0) & (e < chunks))
        def _():
            backward_chunk(e)

        f = c - PLANE_STEPS

        @pl.when((f >= 0) & (f < chunks))
        def _():
            plane_chunk(f)

        @pl.when(f == half)
        def _():
            lat_begin(0)

        @pl.when(f == half + SUM_STEPS)
        def _():
            lat_end(0)

        @pl.when(f == chunks)
        def _():
            lat_begin(1)
            pairs()

        @pl.when(f == chunks + SUM_STEPS)
        def _():
            lat_end(1)

        return carry

    ticks = chunks + (gz_count - 1) * HOP_STEPS + max(LATE_STEPS, PLANE_STEPS + SUM_STEPS + 1)
    lax.fori_loop(0, ticks, tick, 0)

    gim = dot(pair_turned[...], out_map, 1, 0) + dot(fw[...], ap[...], 1, 1)
    gim_ref[...] = gim.astype(BF16)
    gf = dot(mix_turned, gr[...], 1, 0) + dot(in_map, ap[...], 1, 0)
    gf_ref[...] = (wc[...] * gf + vecs[3:4, :] * grad[...]).astype(BF16)

    for group in range(2):
        gz_all(group).wait_recv()
        packed = jnp.sum(gk2[group], axis=0) * (1.0 / math.sqrt(row_total))
        for tap in range(taps):
            for tile in range(part):
                place = tap * part + tile
                lane = (group * part + tile) * 128
                gk_ref[tap : tap + 1, lane : lane + 128] = packed[place : place + 1, :]

    for group in range(2):
        lat_all(group).wait_send()
        gz_all(group).wait_send()
    pltpu.make_async_remote_copy(
        src_ref=gsend.at[pl.ds(0, lat_count - 1)], dst_ref=grecv.at[pl.ds(0, lat_count - 1)],
        send_sem=gs_sem, recv_sem=gr_sem, device_id=(gz, me), device_id_type=MESH,
    ).wait_send()

    def drain(c, carry):
        lanes = span(c)
        pltpu.make_async_remote_copy(
            src_ref=osend.at[pl.ds(0, lat_count - 1), :, lanes],
            dst_ref=orecv.at[pl.ds(1, lat_count - 1), :, lanes],
            send_sem=os_sem.at[c], recv_sem=or_sem.at[c], device_id=(gz, me), device_id_type=MESH,
        ).wait_send()

        @pl.when(gz < gz_count - 1)
        def _():
            forward_copy(c).wait_send()

        @pl.when(gz > 0)
        def _():
            backward_copy(c).wait_send()

        return carry

    lax.fori_loop(0, chunks, drain, 0)


def write_out(*refs):
    sources, results, sem = refs[:5], refs[5:10], refs[10]
    copies = [
        pltpu.make_async_copy(source, result, sem.at[place])
        for place, (source, result) in enumerate(zip(sources, results))
    ]
    for copy in copies:
        copy.start()
    for copy in copies:
        copy.wait()


def per_device(
    features, input_map, output_map, step_size, decay_rate, skip_gain, kernel, cotangent
):
    columns, sections, channels = features.shape
    assert columns == 1
    heads = step_size.shape[2]
    states = input_map.shape[2]
    taps = kernel.shape[0]
    assert taps == 3
    gz_count = lax.axis_size("gz")
    lat_count = lax.axis_size("lat")
    extent, rows, _ = cotangent.shape
    assert extent == lat_count
    width = 256
    chunks = channels // width
    row_total = columns * sections * gz_count * lat_count
    vmem = pl.BlockSpec(memory_space=pltpu.VMEM)
    hbm = pl.BlockSpec(memory_space=pl.ANY)
    full = (sections, channels)
    turned = (states, channels)
    held = pl.pallas_call(
        functools.partial(kernel_body, gz_count, lat_count, width, row_total),
        out_shape=(
            pltpu.VMEM(cotangent.shape, BF16),
            pltpu.VMEM(full, BF16),
            pltpu.VMEM((sections, states), BF16),
            pltpu.VMEM((sections, states), BF16),
            pltpu.VMEM((taps, channels), F32),
        ),
        in_specs=[hbm] * 8,
        out_specs=(vmem,) * 5,
        scratch_shapes=[
            pltpu.VMEM(full, BF16),
            pltpu.VMEM((extent + 2, rows, channels), BF16),
            pltpu.VMEM((lat_count, rows, channels), BF16),
            pltpu.VMEM((lat_count, rows, channels), BF16),
            pltpu.VMEM((lat_count, rows, channels), BF16),
            pltpu.VMEM((extent + 2, rows, channels), BF16),
            pltpu.VMEM((sections, width), F32),
            pltpu.VMEM(full, BF16),
            pltpu.VMEM(full, BF16),
            pltpu.VMEM(full, F32),
            pltpu.VMEM(full, F32),
            pltpu.VMEM(full, F32),
            pltpu.VMEM(full, F32),
            pltpu.VMEM(turned, F32),
            pltpu.VMEM(turned, F32),
            pltpu.VMEM((chunks, states, width), BF16),
            pltpu.VMEM((chunks, states, width), BF16),
            pltpu.VMEM((chunks, states, width), BF16),
            pltpu.VMEM((chunks, states, width), BF16),
            pltpu.VMEM(turned, BF16),
            pltpu.VMEM(turned, BF16),
            pltpu.VMEM((8, channels), F32),
            pltpu.VMEM((2, lat_count, taps * channels // 256, 128), F32),
            pltpu.VMEM((2, gz_count, taps * channels // 256, 128), F32),
            pltpu.VMEM((sections, sections), BF16),
            pltpu.VMEM((sections, states), BF16),
            pltpu.VMEM((sections, states), BF16),
            pltpu.VMEM((heads, sections), F32),
            pltpu.VMEM((1, heads), F32),
            pltpu.VMEM((1, heads), F32),
            pltpu.VMEM((taps, channels), F32),
            pltpu.SemaphoreType.DMA((8,)),
            pltpu.SemaphoreType.DMA,
            pltpu.SemaphoreType.DMA,
            pltpu.SemaphoreType.DMA((chunks,)),
            pltpu.SemaphoreType.DMA((chunks,)),
            pltpu.SemaphoreType.DMA((chunks,)),
            pltpu.SemaphoreType.DMA((chunks,)),
            pltpu.SemaphoreType.DMA((chunks,)),
            pltpu.SemaphoreType.DMA((chunks,)),
            pltpu.SemaphoreType.DMA((8,)),
        ],
        compiler_params=pltpu.CompilerParams(collective_id=0, has_side_effects=True),
    )(
        features,
        input_map.reshape(sections, states),
        output_map.reshape(sections, states),
        jnp.swapaxes(step_size, 1, 2).reshape(heads, sections),
        decay_rate.reshape(1, heads),
        skip_gain.reshape(1, heads),
        kernel,
        cotangent,
    )
    lateral_out, grad_features, grad_in, grad_out, grad_kernel = pl.pallas_call(
        write_out,
        out_shape=(
            jax.ShapeDtypeStruct(cotangent.shape, BF16),
            jax.ShapeDtypeStruct(full, BF16),
            jax.ShapeDtypeStruct((sections, states), BF16),
            jax.ShapeDtypeStruct((sections, states), BF16),
            jax.ShapeDtypeStruct((taps, channels), F32),
        ),
        in_specs=[vmem] * 5,
        out_specs=(hbm,) * 5,
        scratch_shapes=[pltpu.SemaphoreType.DMA((5,))],
    )(*(pltpu.with_memory_space_constraint(one, pltpu.VMEM) for one in held))
    return (
        lateral_out,
        grad_features.reshape(features.shape),
        grad_in.reshape(input_map.shape),
        grad_out.reshape(output_map.shape),
        grad_kernel,
    )


def solution(mesh):
    in_specs = (
        P("lat", "gz", None),
        P("lat", "gz", None),
        P("lat", "gz", None),
        P("lat", "gz", None),
        P(),
        P(),
        P(),
        P(None, ("gz", "lat"), None),
    )
    out_specs = (
        P(None, ("gz", "lat"), None),
        P("lat", "gz", None),
        P("lat", "gz", None),
        P("lat", "gz", None),
        P(),
    )
    return jax.shard_map(
        per_device, mesh=mesh, in_specs=in_specs, out_specs=out_specs, check_vma=False
    )
```
